512 devices in a mesh: body: 2 (over core), gx: 16 (over y, x), gy: 16 (over z).
Axes of the slice: x: 4, y: 4, z: 16, core: 2. Of those that a mesh axis runs over, the one named last changes fastest.
Arguments:
- surface_disp: float32 [2, 3, 49, 131072], P('body', None, None, ('gx', 'gy')), may hold values from -6 to 6
- proj_coords: float32 [2, 2, 36, 65536], P('body', None, None, ('gx', 'gy')), may hold values from -1 to 1
- pair_slave: int32 [2, 65536], P('body', ('gx', 'gy')), may hold values from 0 to 511
- pair_owner: int32 [2, 65536, 1], P('body', ('gx', 'gy')), may hold values from 0 to 255; in each aligned block of 256 rows (0 to 255, 256 to 511, ..., all dimensions but the last counted through in order) at most 2 rows name the same one
- send_list: int32 [2, 256, 512], P(None, ('gx', 'gy')), may hold values from 0 to 511
Outputs:
- nodal_force: float32 [2, 3, 768, 6144], P('body', None, 'gx', 'gy')
The draws below stay inside these ranges and needn't reach their ends.
Inputs may be any that keep to these rules, and one draw needn't show every extreme that they name: `pair_owner`: within the 256 pairs of one slave tile, at most 2 name the same owner tile; in some tile exactly 2 do.
All inputs are finite; a program needn't handle non-finite values.
Results may differ from the reference program's by a relative error of at most 0.0003.
Values sent between devices are 32-bit elements; how exact they have to be, the bound alone decides.
No kernel may reach another device: no remote copies, remote signals or barrier semaphores. Data moves between devices by JAX's collectives and lax.ppermute only.
A program may use at most 64 MiB of HBM per device.

```python
import math
import jax
import jax.numpy as jnp
import numpy as np
from jax import lax

SX = 8
SY = 64
PAIR_DEV = 256
SEG_DEV = 512
CAP = 2
TILES = 256
SEGS = 131072
PAIRS = 65536
N_GX = 16
N_GY = 16


def plant(array, own_key, smallest, top_value):
    index_at = [jax.random.randint(jax.random.fold_in(own_key, axis), (), 0, length) for axis, length in enumerate(array.shape)]
    main_axis = array.shape.index(max(array.shape))
    next_to = index_at[:main_axis] + [(index_at[main_axis] + 1) % array.shape[main_axis]] + index_at[main_axis + 1:]
    return array.at[tuple(index_at)].set(smallest).at[tuple(next_to)].set(top_value)


def block_levels(own_key, extent, cuts, least, high):
    factor_of = 1.0
    for dim, shards_of in cuts:
        steps = jax.random.uniform(jax.random.fold_in(jax.random.fold_in(own_key, 6), dim), (shards_of,), jnp.float32, least / len(cuts), high / len(cuts))
        factor_of = factor_of * jnp.repeat(jnp.exp(steps), extent[dim] // shards_of).reshape((-1,) + (1,) * (len(extent) - 1 - dim))
    return factor_of


def assign_block(own_key, own, number, rows, number_of, top, limit, lean):
    order = jax.random.permutation(own_key, number_of)
    crowded, common = load_shares(number_of, rows * top, limit, lean, True), load_shares(number_of, rows * top, limit, lean, False)
    places = jnp.arange(number_of)

    def named(tallies, offset_by):
        used = int((tallies > 0).sum())
        fixed = max(1, used // 4)
        passed = fixed + (places - fixed + offset_by * (used - fixed)) % max(1, number_of - fixed)
        return jnp.zeros((number_of,), jnp.int32).at[order[jnp.where(places < fixed, places, passed)]].set(jnp.asarray(tallies, jnp.int32))

    tallies = jnp.where(number % 4 == 0, named(crowded, number // 4), named(common, number - number // 4 - 1))
    mixed = jax.random.permutation(jax.random.fold_in(own, 3), number_of)
    source_of, taker = mixed[0:number_of // 2 * 2:2], mixed[1:number_of // 2 * 2:2]
    margin = jnp.minimum(tallies[source_of] - 1, limit - tallies[taker]) // 2
    margin = jnp.where((source_of == order[0]) | (taker == order[0]) | (tallies[taker] == 0), 0, jnp.maximum(margin, 0))
    passed = jax.random.randint(jax.random.fold_in(own, 4), (number_of // 2,), 0, 1 << 20) % (margin + 1)
    tallies = tallies.at[source_of].add(-passed).at[taker].add(passed)
    labels = jnp.searchsorted(jnp.cumsum(tallies), jnp.arange(rows * top), side="right").astype(jnp.int32)
    table = labels.reshape(top, rows).T
    table = table[jax.random.permutation(jax.random.fold_in(own, 1), rows)]
    offset_by = jax.random.randint(jax.random.fold_in(own, 2), (rows, 1), 0, top)
    return jnp.take_along_axis(table, (jnp.arange(top)[None, :] + offset_by) % top, axis=1)


def load_shares(number_of, total, limit, lean, full):
    weights = [(1 << 20) // math.isqrt(standing ** lean) + 1 for standing in range(1, number_of + 1)]
    largest = limit if full else min(limit, max(-(-total // number_of), total * weights[0] // sum(weights)))
    least = 1 if total - largest >= number_of - 1 else 0
    counts, spare = [largest] + [least] * (number_of - 1), total - largest - least * (number_of - 1)
    while spare > 0:
        movable = [i for i in range(1, number_of) if counts[i] < largest] or [i for i in range(1, number_of) if counts[i] < limit]
        pool, remaining = sum([weights[i] for i in movable]), spare
        for i in movable:
            extra = min(limit - counts[i], max(1, remaining * weights[i] // pool), spare)
            counts[i] = counts[i] + extra
            spare = spare - extra
    return np.array(counts)


def scatter_about(own_key, shape, width, most, split=(), kind=jnp.bfloat16):
    array = width * jax.random.normal(own_key, shape, jnp.float32)
    if split:
        array = array * block_levels(own_key, shape, split, -0.22, 0.18)
    return jnp.clip(array, -most, most).astype(kind)


def setup_inputs(seed: int = 0) -> dict:
    key_of = jax.random.split(jax.random.key(seed), 6)
    surface_disp = scatter_about(key_of[0], (2, 3, 49, SEGS), 1.0, 6.0, ((0, 2), (3, 256)), jnp.float32)
    proj_coords = jnp.clip(jax.random.uniform(key_of[1], (2, 2, 36, PAIRS), jnp.float32, -1.0, 1.0) * block_levels(key_of[1], (2, 2, 36, PAIRS), ((0, 2), (3, 256)), -0.4, 0.0), -1.0, 1.0)
    pair_slave = plant(jax.random.randint(key_of[2], (2, PAIRS), 0, SEG_DEV), jax.random.fold_in(key_of[2], 1), 0, SEG_DEV - 1).astype(jnp.int32)
    pair_owner_keys = jax.random.split(jax.random.fold_in(key_of[3], 1), 2 * PAIRS // PAIR_DEV)
    pair_owner_turns = jax.random.permutation(jax.random.fold_in(key_of[3], 3), 2 * PAIRS // PAIR_DEV)
    pair_owner = jax.vmap(lambda own, number: assign_block(jax.random.fold_in(key_of[3], 2), own, number, PAIR_DEV, TILES, 1, CAP, 2))(pair_owner_keys, pair_owner_turns).reshape((2, PAIRS, 1))
    send_list = plant(jax.random.randint(key_of[4], (2, TILES, TILES * CAP), 0, SEG_DEV), jax.random.fold_in(key_of[4], 1), 0, SEG_DEV - 1).astype(jnp.int32)
    return dict(surface_disp=surface_disp, proj_coords=proj_coords, pair_slave=pair_slave, pair_owner=pair_owner, send_list=send_list)


KAPPA = 2.0
SHEAR = 1.0
LOBATTO_POINTS = (-1.0, -0.8302238962785670, -0.4688487934707142, 0.0, 0.4688487934707142, 0.8302238962785670, 1.0)
GAUSS_POINTS = (-0.9324695142031521, -0.6612093864662645, -0.2386191860831969, 0.2386191860831969, 0.6612093864662645, 0.9324695142031521)
GAUSS_WEIGHTS = (0.1713244923791704, 0.3607615730481386, 0.4679139345726910, 0.4679139345726910, 0.3607615730481386, 0.1713244923791704)


def basis_traced(abscissa):
    points = LOBATTO_POINTS
    factors = []
    for k in range(7):
        product = jnp.ones_like(abscissa)
        for m in range(7):
            if m != k:
                product = product * ((abscissa - points[m]) * (1.0 / (points[k] - points[m])))
        factors.append(product)
    return jnp.stack(factors)


def slave_table():
    single = basis_traced(jnp.asarray(GAUSS_POINTS, jnp.float32)).T
    return (single[:, None, :, None] * single[None, :, None, :]).reshape(36, 49)


def quad_weights():
    weights = jnp.asarray(GAUSS_WEIGHTS, jnp.float32)
    return (weights[:, None] * weights[None, :]).reshape(36)


def pair_forces(slave_nodes, master_nodes, pair_coords, normal_sign):
    highest = lax.Precision.HIGHEST
    slave_basis = slave_table()
    quad_weight = quad_weights()
    first_basis = basis_traced(pair_coords[0])
    second_basis = basis_traced(pair_coords[1])
    slave_value = jnp.einsum("qi,cip->cqp", slave_basis, slave_nodes, precision=highest)
    master_grid = master_nodes.reshape(3, 7, 7, -1)
    partial_sum = jnp.einsum("lqp,cklp->ckqp", second_basis, master_grid, precision=highest)
    master_value = jnp.sum(first_basis[None] * partial_sum, axis=1)
    offset = master_value - slave_value
    normal_gap = normal_sign * offset[2]
    pressure = KAPPA * jax.nn.softplus(-normal_gap)
    traction = jnp.stack([SHEAR * offset[0], SHEAR * offset[1], -normal_sign * pressure]) * quad_weight[None, :, None]
    slave_force = jnp.einsum("qi,cqp->cip", slave_basis, traction, precision=highest)
    weighted = second_basis[None] * traction[:, None]
    master_force = -jnp.einsum("kqp,clqp->cklp", first_basis, weighted, precision=highest).reshape(3, 49, -1)
    return slave_force, master_force


def slot_ranks(owners, tile_count):
    onehot = (owners[:, None] == jnp.arange(tile_count, dtype=jnp.int32)[None, :]).astype(jnp.int32)
    before = jnp.cumsum(onehot, axis=0) - onehot
    return jnp.sum(before * onehot, axis=1).astype(jnp.int32)


def assemble_periodic(element_force):
    segment_grid = element_force.reshape(3, 7, 7, N_GX, N_GY, SX, SY)
    segment_grid = segment_grid.transpose(0, 1, 2, 3, 5, 4, 6).reshape(3, 7, 7, N_GX * SX, N_GY * SY)
    along_x = segment_grid[:, :6].at[:, 0].add(jnp.roll(segment_grid[:, 6], 1, axis=2))
    along_y = along_x[:, :, :6].at[:, :, 0].add(jnp.roll(along_x[:, :, 6], 1, axis=3))
    return along_y.transpose(0, 3, 1, 4, 2).reshape(3, 6 * N_GX * SX, 6 * N_GY * SY)


def reference(surface_disp, proj_coords, pair_slave, pair_owner, send_list):
    tile_count = N_GX * N_GY
    segment_count = SX * SY
    running = (jnp.zeros((3, 49, tile_count * segment_count), jnp.float32),
               jnp.zeros((3, 49, tile_count * segment_count), jnp.float32))
    for body_side in range(2):
        other_side = 1 - body_side
        normal_sign = 1.0 - 2.0 * body_side

        def per_tile(state, tile_index):
            start = tile_index * PAIR_DEV
            slaves = lax.dynamic_slice_in_dim(pair_slave[body_side], start, PAIR_DEV)
            owners = lax.dynamic_slice_in_dim(pair_owner[body_side, :, 0], start, PAIR_DEV)
            pair_coords = lax.dynamic_slice_in_dim(proj_coords[body_side], start, PAIR_DEV, axis=2)
            slot_rank = slot_ranks(owners, tile_count)
            masters = send_list[other_side][owners, tile_index * CAP + slot_rank]
            master_ids = (owners * segment_count + masters).astype(jnp.int32)
            slave_ids = (tile_index * segment_count + slaves).astype(jnp.int32)
            slave_nodes = jnp.take(surface_disp[body_side], slave_ids, axis=2)
            master_nodes = jnp.take(surface_disp[other_side], master_ids, axis=2)
            slave_force, master_force = pair_forces(slave_nodes, master_nodes, pair_coords, normal_sign)
            forces = list(state)
            forces[body_side] = forces[body_side].at[:, :, slave_ids].add(slave_force)
            forces[other_side] = forces[other_side].at[:, :, master_ids].add(master_force)
            return tuple(forces), None

        running, skipped = lax.scan(per_tile, running, jnp.arange(tile_count, dtype=jnp.int32))
    return jnp.stack([assemble_periodic(running[0]), assemble_periodic(running[1])])
```

```python
import jax
import jax.numpy as jnp
import numpy as np
from jax import lax
from jax.experimental import pallas as pl
from jax.experimental.pallas import tpu as pltpu
from jax.sharding import PartitionSpec as P

SX = 8
SY = 64
TILES = 256
KAPPA = 2.0
SHEAR = 1.0
LOBATTO_POINTS = (
    -1.0,
    -0.830223896278567,
    -0.4688487934707142,
    0.0,
    0.4688487934707142,
    0.830223896278567,
    1.0,
)
GAUSS_POINTS = (
    -0.932469514203152,
    -0.6612093864662645,
    -0.2386191860831969,
    0.2386191860831969,
    0.6612093864662645,
    0.932469514203152,
)
GAUSS_WEIGHTS = (
    0.1713244923791704,
    0.3607615730481386,
    0.467913934572691,
    0.467913934572691,
    0.3607615730481386,
    0.1713244923791704,
)
F32 = jnp.float32
BF16 = jnp.bfloat16
HIGHEST = lax.Precision.HIGHEST
NN = (((1,), (0,)), ((), ()))
NT = (((1,), (1,)), ((), ()))


def lagrange_scales():
    scales = []
    for k in range(7):
        product = 1.0
        for m in range(7):
            if m != k:
                product /= LOBATTO_POINTS[k] - LOBATTO_POINTS[m]
        scales.append(product)
    return scales


def tables():
    points = np.array(LOBATTO_POINTS)
    gauss = np.array(GAUSS_POINTS)
    single = np.ones((6, 7))
    for k in range(7):
        for m in range(7):
            if m != k:
                single[:, k] *= (gauss - points[m]) / (points[k] - points[m])
    basis = np.einsum("ak,bm->abkm", single, single).reshape(36, 49)
    to_points = np.zeros((120, 192), np.float32)
    to_nodes = np.zeros((192, 120), np.float32)
    for c in range(3):
        to_points[40 * c : 40 * c + 36, 49 * c : 49 * c + 49] = basis
    for row in range(192):
        c, k, m = node_of_row(row)
        to_nodes[row, 40 * c : 40 * c + 36] = basis[:, 7 * k + m]
    spread = np.zeros((512, 384), np.float32)
    for g in range(8):
        for lc in range(64):
            y = 6 * lc + g if g < 7 else (0 if lc == 63 else -1)
            if 0 <= y < 384:
                spread[64 * g + lc, y] = 1.0
    stack = np.zeros((144, 216), np.float32)
    for la in range(9):
        for j in range(24):
            if la < 8 and j < 21:
                c, x = j // 7, 6 * la + j % 7
            elif la == 8 and j >= 21:
                c, x = j - 21, 0
            else:
                continue
            if x < 48:
                stack[48 * c + x, 24 * la + j] = 1.0
    return (
        jnp.asarray(to_points),
        jnp.asarray(to_nodes),
        jnp.asarray(spread, BF16),
        jnp.asarray(stack, BF16),
    )


def node_of_row(row):
    g, j = divmod(row, 24)
    m = min(g, 6)
    if j < 21:
        return j // 7, j % 7, m
    return j - 21, 6, m


def rows_of_node(c, k, m):
    rows = [24 * m + 7 * c + k]
    if k == 6:
        rows.append(24 * m + 21 + c)
    if m == 6:
        rows.append(168 + 7 * c + k)
    if k == 6 and m == 6:
        rows.append(189 + c)
    return rows


def split(value):
    high = value.astype(BF16)
    return high, (value - high.astype(F32)).astype(BF16)


def dot(a, b, dims):
    return lax.dot_general(a, b, dims, preferred_element_type=F32)


def onehot(condition):
    return jnp.where(condition, 1.0, 0.0).astype(BF16)


def iota(shape, dim):
    return lax.broadcasted_iota(jnp.int32, shape, dim)


def load_surface(surf_ref, scratch):
    scratch[144:, :] = jnp.zeros((scratch.shape[0] - 144, 512), F32)
    for j in range(4):
        scratch[0:147, 128 * j : 128 * j + 128] = surf_ref[pl.ds(j, 147, stride=4), :]


def gather_kernel(body_ref, list_ref, surf_ref, out_ref, surf_scr, rows_scr):
    mine = jnp.where(body_ref[0] == 0, list_ref[0], list_ref[1])
    column = jnp.transpose(jnp.broadcast_to(mine.astype(F32), (8, 512)))[:, 0:1]
    pick = onehot(column.astype(jnp.int32) == iota((512, 512), 1))
    load_surface(surf_ref, surf_scr)
    high, low = split(surf_scr[...])
    rows = dot(pick, high, NT) + dot(pick, low, NT)
    rows_scr[0] = rows[:, :128]
    rows_scr[1] = rows[:, 128:]
    left = iota((256, 128), 1) < 64
    out_ref[:, 0:128] = rows_scr[0, pl.ds(0, 256, stride=2), :]
    out_ref[:, 128:256] = rows_scr[0, pl.ds(1, 256, stride=2), :]
    out_ref[:, 256:384] = jnp.where(
        left,
        rows_scr[1, pl.ds(0, 256, stride=2), :],
        pltpu.roll(rows_scr[1, pl.ds(1, 256, stride=2), :], 64, 1),
    )


def slave_kernel(surf_ref, slave_ref, coord_ref, owner_ref, table_ref, out_ref, surf_scr):
    load_surface(surf_ref, surf_scr)
    at_points = lax.dot_general(
        table_ref[...], surf_scr[...], NN, precision=HIGHEST, preferred_element_type=F32
    )
    pick = onehot(iota((512, 256), 0) == slave_ref[...])
    high, low = split(at_points)
    out_ref[0:120, :] = dot(high, pick, NN) + dot(low, pick, NN)
    out_ref[120:200, :] = jnp.zeros((80, 256), F32)
    for e in range(2):
        for j in range(2):
            out_ref[120 + 40 * e : 156 + 40 * e, 128 * j : 128 * j + 128] = coord_ref[
                pl.ds(2 * j + e, 36, stride=4), :
            ]
    out_ref[200:208, :] = jnp.broadcast_to(owner_ref[...].astype(F32), (8, 256))


def unpack(buffer):
    turned = [jnp.transpose(buffer[:, 128 * i : 128 * i + 128]) for i in range(3)]
    return (
        jnp.concatenate([turned[0], turned[2][:64]], axis=0),
        jnp.concatenate([turned[1], turned[2][64:]], axis=0),
    )


def pair_kernel(
    sign_ref, buffer_ref, pack_ref, out_ref, traction_ref, master_scr, basis_scr, force_scr
):
    sign = sign_ref[0]
    owner = pack_ref[200:201, :].astype(jnp.int32)
    named = owner == iota((256, 256), 0)
    pick = onehot(named)
    earlier = onehot(iota((256, 256), 0) < iota((256, 256), 1))
    before = dot(pick, earlier, NN)
    picks = [onehot(named & (before < 0.5)), onehot(named & (before > 0.5))]
    master = jnp.zeros((192, 256), F32)
    for half, chosen in zip(unpack(buffer_ref[...]), picks):
        high, low = split(half)
        master = master + dot(high, chosen, NN) + dot(low, chosen, NN)
    master_scr[...] = master
    scales = lagrange_scales()
    for e in range(2):
        coord = pack_ref[120 + 40 * e : 160 + 40 * e, :]
        parts = [coord - point for point in LOBATTO_POINTS]
        prefix = [None, parts[0]]
        for i in range(1, 6):
            prefix.append(prefix[-1] * parts[i])
        suffix = [None] * 7
        suffix[5] = parts[6]
        for i in range(4, -1, -1):
            suffix[i] = suffix[i + 1] * parts[i + 1]
        for k in range(7):
            if k == 0:
                value = suffix[0]
            elif k == 6:
                value = prefix[6]
            else:
                value = prefix[k] * suffix[k]
            basis_scr[e, k] = value * scales[k]
    point = iota((8, 128), 0)
    for t in range(5):
        q = point + 8 * t
        a = jnp.zeros((8, 128), jnp.int32)
        for i in range(1, 6):
            a = a + jnp.where(q >= 6 * i, 1, 0)
        b = q - 6 * a
        weight = jnp.ones((8, 128), F32)
        for index in (a, b):
            near = jnp.where(index > 2, 5 - index, index)
            weight = weight * jnp.where(
                near == 0,
                GAUSS_WEIGHTS[0],
                jnp.where(near == 1, GAUSS_WEIGHTS[1], GAUSS_WEIGHTS[2]),
            )
        weight = jnp.where(q < 36, weight, 0.0)
        rows = slice(8 * t, 8 * t + 8)
        for j in range(2):
            lanes = slice(128 * j, 128 * j + 128)
            first = [basis_scr[0, k, rows, lanes] for k in range(7)]
            second = [basis_scr[1, k, rows, lanes] for k in range(7)]
            for c in range(3):
                total = None
                for k in range(7):
                    inner = None
                    for m in range(7):
                        i = 49 * c + 7 * k + m
                        term = second[m] * master_scr[i : i + 1, lanes]
                        inner = term if inner is None else inner + term
                    inner = first[k] * inner
                    total = inner if total is None else total + inner
                offset = total - pack_ref[40 * c + 8 * t : 40 * c + 8 * t + 8, lanes]
                if c < 2:
                    traction = SHEAR * offset
                else:
                    v = -(sign * offset)
                    pressure = jnp.maximum(v, 0.0) + jnp.log1p(jnp.exp(-jnp.abs(v)))
                    traction = -sign * (KAPPA * pressure)
                traction_ref[40 * c + 8 * t : 40 * c + 8 * t + 8, lanes] = weight * traction
    force_scr[192:256, :] = jnp.zeros((64, 256), F32)
    for j in range(2):
        lanes = slice(128 * j, 128 * j + 128)
        for k in range(7):
            first = basis_scr[0, k, :, lanes]
            weighted = [-first * traction_ref[40 * c : 40 * c + 40, lanes] for c in range(3)]
            for m in range(7):
                second = basis_scr[1, m, :, lanes]
                for c in range(3):
                    row = jnp.sum(weighted[c] * second, axis=0, keepdims=True)
                    for at in rows_of_node(c, k, m):
                        force_scr[at : at + 1, lanes] = row
    high, low = split(force_scr[...])
    to_owner = [dot(chosen, high, NT) + dot(chosen, low, NT) for chosen in picks]
    lane = iota((256, 128), 1)
    row = iota((256, 128), 0)
    wrap = (row & 15) == 0

    def shift_x(value):
        return jnp.concatenate([value[240:], value[:240]], axis=0)

    def shift_y(value):
        return jnp.where(wrap, pltpu.roll(value, 241, 0), pltpu.roll(value, 1, 0))

    rim = jnp.zeros((256, 128), jnp.bool_)
    for g in range(6):
        rim = rim | ((lane >= 24 * g + 21) & (lane < 24 * g + 24))
    tails = []
    for r in range(2):
        head = to_owner[r][:, :128]
        out_ref[:, 128 * r : 128 * r + 128] = jnp.where(rim, shift_x(head), head)
        tail = to_owner[r][:, 128:]
        tail = jnp.where(lane >= 40, shift_y(tail), tail)
        edge = ((lane >= 13) & (lane < 16)) | ((lane >= 37) & (lane < 40)) | (lane >= 61)
        tails.append(jnp.where(edge, shift_x(tail), tail))
    out_ref[:, 256:384] = jnp.where(lane < 64, tails[0], pltpu.roll(tails[1], 64, 1))


def slave_force_kernel(traction_ref, slave_ref, table_ref, own_ref, x_ref, y_ref, xy_ref):
    force = lax.dot_general(
        table_ref[...], traction_ref[...], NN, precision=HIGHEST, preferred_element_type=F32
    )
    pick = onehot(iota((512, 256), 0) == slave_ref[...])
    high, low = split(force)
    element = dot(high, pick, NT) + dot(low, pick, NT)
    own_ref[...] = element[:168]
    x_ref[...] = element[:168, 384:]
    y_ref[...] = element[168:]
    xy_ref[...] = element[168:, 384:]


def assemble_kernel(
    body_ref,
    buffer_ref,
    list_ref,
    list_x_ref,
    list_y_ref,
    list_xy_ref,
    own_ref,
    x_ref,
    y_ref,
    xy_ref,
    spread_ref,
    stack_ref,
    out_ref,
    column_scr,
    place_scr,
):
    on_first = body_ref[0] == 0
    sub = iota((8, 512), 0)
    lists = jnp.zeros((8, 512), jnp.int32)
    for i, ref in enumerate((list_ref, list_x_ref, list_y_ref, list_xy_ref)):
        lists = jnp.where(sub == i, jnp.where(on_first, ref[0], ref[1]), lists)
    column_scr[:, 0:8] = jnp.transpose(lists.astype(F32))
    columns = [
        column_scr[pl.ds(r, 256, stride=2), :][:, 0:8].astype(jnp.int32) for r in range(2)
    ]
    columns = jnp.concatenate(columns, axis=0)
    near = iota((512, 512), 1)
    far = iota((512, 128), 1)
    far = jnp.where(far < 64, far + 448, -1)
    halves = unpack(buffer_ref[...])
    element = []
    for i, rows in ((0, slice(0, 168)), (2, slice(168, 192))):
        data = jnp.concatenate([half[rows] for half in halves], axis=1)
        high, low = split(data)
        inside = onehot(columns[:, i : i + 1] == near)
        outside = onehot(columns[:, i + 1 : i + 2] == far)
        element.append(
            (
                dot(high, inside, NN) + dot(low, inside, NN),
                dot(high, outside, NN) + dot(low, outside, NN),
            )
        )
    inside = jnp.concatenate([element[0][0] + own_ref[...], element[1][0] + y_ref[...]], axis=0)
    outside = jnp.concatenate(
        [
            element[0][1] + pltpu.roll(x_ref[...], 64, 1),
            element[1][1] + pltpu.roll(xy_ref[...], 64, 1),
        ],
        axis=0,
    )
    left = iota((24, 128), 1) < 64
    for la in range(9):
        if la == 8:
            block = outside
        else:
            block = inside[:, 128 * (la // 2) : 128 * (la // 2) + 128]
        for pair in range(4):
            first = block[48 * pair : 48 * pair + 24]
            second = block[48 * pair + 24 : 48 * pair + 48]
            if la % 2 == 0:
                second = pltpu.roll(second, 64, 1)
            else:
                first = pltpu.roll(first, 64, 1)
            place_scr[24 * la : 24 * la + 24, 128 * pair : 128 * pair + 128] = jnp.where(
                left, first, second
            )
    high, low = split(place_scr[...])
    spread = spread_ref[...]
    high, low = split(dot(high, spread, NN) + dot(low, spread, NN))
    stack = stack_ref[...]
    out_ref[...] = dot(stack, high, NN) + dot(stack, low, NN)


def call(kernel, outs, spaces, scratch, name):
    smem = pl.BlockSpec(memory_space=pltpu.SMEM)
    vmem = pl.BlockSpec(memory_space=pltpu.VMEM)
    shapes = [jax.ShapeDtypeStruct(shape, F32) for shape in outs]
    return pl.pallas_call(
        kernel,
        out_shape=shapes if len(shapes) > 1 else shapes[0],
        in_specs=[smem if space == "s" else vmem for space in spaces],
        out_specs=[vmem] * len(shapes) if len(shapes) > 1 else vmem,
        scratch_shapes=[pltpu.VMEM(shape, F32) for shape in scratch],
        name=name,
    )


def cross_body(value):
    return lax.ppermute(value, "body", [(0, 1), (1, 0)])


def across_tiles(buffer):
    return lax.all_to_all(buffer, ("gx", "gy"), split_axis=0, concat_axis=0, tiled=True)


def from_behind(value, by_x, by_y):
    pairs = []
    for x in range(16):
        for y in range(16):
            pairs.append((16 * x + y, 16 * ((x + by_x) % 16) + (y + by_y) % 16))
    return lax.ppermute(value, ("gx", "gy"), pairs)


def local(surface_disp, proj_coords, pair_slave, pair_owner, send_list):
    to_points, to_nodes, spread, stack = tables()
    side = lax.axis_index("body")
    body = side.astype(jnp.int32).reshape(1)
    sign = (2.0 * side.astype(F32) - 1.0).reshape(1)
    surface = surface_disp.reshape(588, 128)
    coords = proj_coords.reshape(2, 36, 2, 128).transpose(1, 2, 0, 3).reshape(144, 128)
    owner = pair_owner.reshape(1, 256)
    outgoing = call(
        gather_kernel, [(256, 384)], "svv", [(256, 512), (2, 512, 128)], "gather"
    )(body, send_list, surface)
    arrived = across_tiles(outgoing)
    packed = call(slave_kernel, [(208, 256)], "vvvvv", [(192, 512)], "slave")(
        surface, pair_slave, coords, owner, to_points
    )
    packed = cross_body(packed)
    list_x = from_behind(send_list, 1, 0)
    list_y = from_behind(send_list, 0, 1)
    list_xy = from_behind(send_list, 1, 1)
    returning, traction = call(
        pair_kernel,
        [(256, 384), (120, 256)],
        "svv",
        [(192, 256), (2, 7, 40, 256), (256, 256)],
        "pairs",
    )(sign, arrived, packed)
    returned = across_tiles(returning)
    own, rim_x, rim_y, rim_xy = call(
        slave_force_kernel,
        [(168, 512), (168, 128), (24, 512), (24, 128)],
        "vvv",
        [],
        "slave_force",
    )(cross_body(traction), pair_slave, to_nodes)
    nodal = call(
        assemble_kernel, [(144, 384)], "s" + "v" * 11, [(512, 128), (216, 512)], "assemble"
    )(
        body,
        returned,
        send_list,
        list_x,
        list_y,
        list_xy,
        own,
        from_behind(rim_x, 1, 0),
        from_behind(rim_y, 0, 1),
        from_behind(rim_xy, 1, 1),
        spread,
        stack,
    )
    return nodal.reshape(1, 3, 48, 384)


def solution(mesh):
    return jax.shard_map(
        local,
        mesh=mesh,
        in_specs=(
            P("body", None, None, ("gx", "gy")),
            P("body", None, None, ("gx", "gy")),
            P("body", ("gx", "gy")),
            P("body", ("gx", "gy"), None),
            P(None, ("gx", "gy"), None),
        ),
        out_specs=P("body", None, "gx", "gy"),
        check_vma=False,
    )
```

```python
import jax
import jax.numpy as jnp
import numpy as np
from jax import lax
from jax.experimental import pallas as pl
from jax.experimental.pallas import tpu as pltpu
from jax.sharding import PartitionSpec as P

SX = 8
SY = 64
TILES = 256
KAPPA = 2.0
SHEAR = 1.0
LOBATTO_POINTS = (
    -1.0,
    -0.830223896278567,
    -0.4688487934707142,
    0.0,
    0.4688487934707142,
    0.830223896278567,
    1.0,
)
GAUSS_POINTS = (
    -0.932469514203152,
    -0.6612093864662645,
    -0.2386191860831969,
    0.2386191860831969,
    0.6612093864662645,
    0.932469514203152,
)
GAUSS_WEIGHTS = (
    0.1713244923791704,
    0.3607615730481386,
    0.467913934572691,
    0.467913934572691,
    0.3607615730481386,
    0.1713244923791704,
)
F32 = jnp.float32
BF16 = jnp.bfloat16
HIGHEST = lax.Precision.HIGHEST
NN = (((1,), (0,)), ((), ()))
NT = (((1,), (1,)), ((), ()))


def lagrange_scales():
    scales = []
    for k in range(7):
        product = 1.0
        for m in range(7):
            if m != k:
                product /= LOBATTO_POINTS[k] - LOBATTO_POINTS[m]
        scales.append(product)
    return scales


def tables():
    points = np.array(LOBATTO_POINTS)
    gauss = np.array(GAUSS_POINTS)
    single = np.ones((6, 7))
    for k in range(7):
        for m in range(7):
            if m != k:
                single[:, k] *= (gauss - points[m]) / (points[k] - points[m])
    basis = np.einsum("ak,bm->abkm", single, single).reshape(36, 49)
    to_points = np.zeros((120, 192), np.float32)
    to_nodes = np.zeros((192, 120), np.float32)
    for c in range(3):
        to_points[40 * c : 40 * c + 36, 49 * c : 49 * c + 49] = basis
    for row in range(192):
        c, k, m = node_of_row(row)
        to_nodes[row, 40 * c : 40 * c + 36] = basis[:, 7 * k + m]
    spread = np.zeros((512, 384), np.float32)
    for g in range(8):
        for lc in range(64):
            y = 6 * lc + g if g < 7 else (0 if lc == 63 else -1)
            if 0 <= y < 384:
                spread[64 * g + lc, y] = 1.0
    stack = np.zeros((144, 216), np.float32)
    for la in range(9):
        for j in range(24):
            if la < 8 and j < 21:
                c, x = j // 7, 6 * la + j % 7
            elif la == 8 and j >= 21:
                c, x = j - 21, 0
            else:
                continue
            if x < 48:
                stack[48 * c + x, 24 * la + j] = 1.0
    return (
        jnp.asarray(to_points),
        jnp.asarray(to_nodes),
        jnp.asarray(spread, BF16),
        jnp.asarray(stack, BF16),
    )


def node_of_row(row):
    g, j = divmod(row, 24)
    m = min(g, 6)
    if j < 21:
        return j // 7, j % 7, m
    return j - 21, 6, m


def rows_of_node(c, k, m):
    rows = [24 * m + 7 * c + k]
    if k == 6:
        rows.append(24 * m + 21 + c)
    if m == 6:
        rows.append(168 + 7 * c + k)
    if k == 6 and m == 6:
        rows.append(189 + c)
    return rows


def split(value):
    high = value.astype(BF16)
    return high, (value - high.astype(F32)).astype(BF16)


def dot(a, b, dims):
    return lax.dot_general(a, b, dims, preferred_element_type=F32)


def onehot(condition):
    return jnp.where(condition, 1.0, 0.0).astype(BF16)


def iota(shape, dim):
    return lax.broadcasted_iota(jnp.int32, shape, dim)


def third(i):
    return pl.ds(i, 256, stride=3)


def load_surface(surf_ref, scratch):
    flat_ref = surf_ref.reshape(588, 128)
    scratch[144:, :] = jnp.zeros((scratch.shape[0] - 144, 512), F32)
    for j in range(4):
        scratch[0:147, 128 * j : 128 * j + 128] = flat_ref[pl.ds(j, 147, stride=4), :]


def gather_kernel(body_ref, list_ref, surf_ref, out_ref, surf_scr, rows_scr):
    mine = jnp.where(body_ref[0] == 0, list_ref[0], list_ref[1])
    column = jnp.transpose(jnp.broadcast_to(mine.astype(F32), (8, 512)))[:, 0:1]
    pick = onehot(column.astype(jnp.int32) == iota((512, 512), 1))
    load_surface(surf_ref, surf_scr)
    high, low = split(surf_scr[...])
    rows = dot(pick, high, NT) + dot(pick, low, NT)
    rows_scr[0] = rows[:, :128]
    rows_scr[1] = rows[:, 128:]
    left = iota((256, 128), 1) < 64
    out_ref[third(0), :] = rows_scr[0, pl.ds(0, 256, stride=2), :]
    out_ref[third(1), :] = rows_scr[0, pl.ds(1, 256, stride=2), :]
    out_ref[third(2), :] = jnp.where(
        left,
        rows_scr[1, pl.ds(0, 256, stride=2), :],
        pltpu.roll(rows_scr[1, pl.ds(1, 256, stride=2), :], 64, 1),
    )


def slave_kernel(surf_ref, slave_ref, coord_ref, owner_ref, table_ref, out_ref, surf_scr):
    load_surface(surf_ref, surf_scr)
    at_points = lax.dot_general(
        table_ref[...], surf_scr[...], NN, precision=HIGHEST, preferred_element_type=F32
    )
    pick = onehot(iota((512, 256), 0) == slave_ref[...])
    high, low = split(at_points)
    out_ref[0:120, :] = dot(high, pick, NN) + dot(low, pick, NN)
    out_ref[120:200, :] = jnp.zeros((80, 256), F32)
    for e in range(2):
        for j in range(2):
            out_ref[120 + 40 * e : 156 + 40 * e, 128 * j : 128 * j + 128] = coord_ref[
                pl.ds(2 * j + e, 36, stride=4), :
            ]
    out_ref[200:208, :] = jnp.where(
        iota((8, 256), 0) == 0, owner_ref[...], slave_ref[...]
    ).astype(F32)


def unpack(buffer_ref):
    turned = [jnp.transpose(buffer_ref[third(i), :]) for i in range(3)]
    return (
        jnp.concatenate([turned[0], turned[2][:64]], axis=0),
        jnp.concatenate([turned[1], turned[2][64:]], axis=0),
    )


def pair_kernel(
    sign_ref, buffer_ref, pack_ref, out_ref, traction_ref, master_scr, basis_scr, force_scr
):
    sign = sign_ref[0]
    owner = pack_ref[200:201, :].astype(jnp.int32)
    named = owner == iota((256, 256), 0)
    pick = onehot(named)
    earlier = onehot(iota((256, 256), 0) < iota((256, 256), 1))
    before = dot(pick, earlier, NN)
    picks = [onehot(named & (before < 0.5)), onehot(named & (before > 0.5))]
    master = jnp.zeros((192, 256), F32)
    for half, chosen in zip(unpack(buffer_ref), picks):
        high, low = split(half)
        master = master + dot(high, chosen, NN) + dot(low, chosen, NN)
    master_scr[...] = master
    scales = lagrange_scales()
    for e in range(2):
        coord = pack_ref[120 + 40 * e : 160 + 40 * e, :]
        parts = [coord - point for point in LOBATTO_POINTS]
        prefix = [None, parts[0]]
        for i in range(1, 6):
            prefix.append(prefix[-1] * parts[i])
        suffix = [None] * 7
        suffix[5] = parts[6]
        for i in range(4, -1, -1):
            suffix[i] = suffix[i + 1] * parts[i + 1]
        for k in range(7):
            if k == 0:
                value = suffix[0]
            elif k == 6:
                value = prefix[6]
            else:
                value = prefix[k] * suffix[k]
            basis_scr[e, k] = value * scales[k]
    point = iota((8, 128), 0)
    for t in range(5):
        q = point + 8 * t
        a = jnp.zeros((8, 128), jnp.int32)
        for i in range(1, 6):
            a = a + jnp.where(q >= 6 * i, 1, 0)
        b = q - 6 * a
        weight = jnp.ones((8, 128), F32)
        for index in (a, b):
            near = jnp.where(index > 2, 5 - index, index)
            weight = weight * jnp.where(
                near == 0,
                GAUSS_WEIGHTS[0],
                jnp.where(near == 1, GAUSS_WEIGHTS[1], GAUSS_WEIGHTS[2]),
            )
        weight = jnp.where(q < 36, weight, 0.0)
        rows = slice(8 * t, 8 * t + 8)
        for j in range(2):
            lanes = slice(128 * j, 128 * j + 128)
            first = [basis_scr[0, k, rows, lanes] for k in range(7)]
            second = [basis_scr[1, k, rows, lanes] for k in range(7)]
            for c in range(3):
                total = None
                for k in range(7):
                    inner = None
                    for m in range(7):
                        i = 49 * c + 7 * k + m
                        term = second[m] * master_scr[i : i + 1, lanes]
                        inner = term if inner is None else inner + term
                    inner = first[k] * inner
                    total = inner if total is None else total + inner
                offset = total - pack_ref[40 * c + 8 * t : 40 * c + 8 * t + 8, lanes]
                if c < 2:
                    traction = SHEAR * offset
                else:
                    v = -(sign * offset)
                    pressure = jnp.maximum(v, 0.0) + jnp.log1p(jnp.exp(-jnp.abs(v)))
                    traction = -sign * (KAPPA * pressure)
                traction_ref[40 * c + 8 * t : 40 * c + 8 * t + 8, lanes] = weight * traction
    force_scr[192:256, :] = jnp.zeros((64, 256), F32)
    for j in range(2):
        lanes = slice(128 * j, 128 * j + 128)
        for k in range(7):
            first = basis_scr[0, k, :, lanes]
            weighted = [-first * traction_ref[40 * c : 40 * c + 40, lanes] for c in range(3)]
            for m in range(7):
                second = basis_scr[1, m, :, lanes]
                for c in range(3):
                    row = jnp.sum(weighted[c] * second, axis=0, keepdims=True)
                    for at in rows_of_node(c, k, m):
                        force_scr[at : at + 1, lanes] = row
    high, low = split(force_scr[...])
    to_owner = [dot(chosen, high, NT) + dot(chosen, low, NT) for chosen in picks]
    lane = iota((256, 128), 1)
    row = iota((256, 128), 0)
    wrap = (row & 15) == 0

    def shift_x(value):
        return jnp.concatenate([value[240:], value[:240]], axis=0)

    def shift_y(value):
        return jnp.where(wrap, pltpu.roll(value, 241, 0), pltpu.roll(value, 1, 0))

    rim = jnp.zeros((256, 128), jnp.bool_)
    for g in range(6):
        rim = rim | ((lane >= 24 * g + 21) & (lane < 24 * g + 24))
    tails = []
    for r in range(2):
        head = to_owner[r][:, :128]
        out_ref[third(r), :] = jnp.where(rim, shift_x(head), head)
        tail = to_owner[r][:, 128:]
        tail = jnp.where(lane >= 40, shift_y(tail), tail)
        edge = ((lane >= 13) & (lane < 16)) | ((lane >= 37) & (lane < 40)) | (lane >= 61)
        tails.append(jnp.where(edge, shift_x(tail), tail))
    out_ref[third(2), :] = jnp.where(lane < 64, tails[0], pltpu.roll(tails[1], 64, 1))


def slave_force_kernel(traction_ref, pack_ref, table_ref, own_ref, x_ref, y_ref, xy_ref):
    force = lax.dot_general(
        table_ref[...], traction_ref[...], NN, precision=HIGHEST, preferred_element_type=F32
    )
    pick = onehot(iota((512, 256), 0) == pack_ref[201:202, :].astype(jnp.int32))
    high, low = split(force)
    element = dot(high, pick, NT) + dot(low, pick, NT)
    own_ref[...] = element[:168]
    x_ref[...] = element[:168, 384:]
    y_ref[...] = element[168:]
    xy_ref[...] = element[168:, 384:]


def column_kernel(
    body_ref, list_ref, list_x_ref, list_y_ref, list_xy_ref, out_ref, column_scr
):
    on_first = body_ref[0] == 0
    sub = iota((8, 512), 0)
    lists = jnp.zeros((8, 512), jnp.int32)
    for i, ref in enumerate((list_ref, list_x_ref, list_y_ref, list_xy_ref)):
        lists = jnp.where(sub == i, jnp.where(on_first, ref[0], ref[1]), lists)
    column_scr[:, 0:8] = jnp.transpose(lists.astype(F32))
    for r in range(2):
        out_ref[256 * r : 256 * r + 256, :] = column_scr[pl.ds(r, 256, stride=2), :]


def assemble_kernel(
    buffer_ref,
    column_ref,
    own_ref,
    x_ref,
    y_ref,
    xy_ref,
    spread_ref,
    stack_ref,
    out_ref,
    place_scr,
):
    columns = column_ref[:, 0:8].astype(jnp.int32)
    near = iota((512, 512), 1)
    far = iota((512, 128), 1)
    far = jnp.where(far < 64, far + 448, -1)
    halves = unpack(buffer_ref)
    element = []
    for i, rows in ((0, slice(0, 168)), (2, slice(168, 192))):
        data = jnp.concatenate([half[rows] for half in halves], axis=1)
        high, low = split(data)
        inside = onehot(columns[:, i : i + 1] == near)
        outside = onehot(columns[:, i + 1 : i + 2] == far)
        element.append(
            (
                dot(high, inside, NN) + dot(low, inside, NN),
                dot(high, outside, NN) + dot(low, outside, NN),
            )
        )
    inside = jnp.concatenate([element[0][0] + own_ref[...], element[1][0] + y_ref[...]], axis=0)
    outside = jnp.concatenate(
        [
            element[0][1] + pltpu.roll(x_ref[...], 64, 1),
            element[1][1] + pltpu.roll(xy_ref[...], 64, 1),
        ],
        axis=0,
    )
    left = iota((24, 128), 1) < 64
    for la in range(9):
        if la == 8:
            block = outside
        else:
            block = inside[:, 128 * (la // 2) : 128 * (la // 2) + 128]
        for pair in range(4):
            first = block[48 * pair : 48 * pair + 24]
            second = block[48 * pair + 24 : 48 * pair + 48]
            if la % 2 == 0:
                second = pltpu.roll(second, 64, 1)
            else:
                first = pltpu.roll(first, 64, 1)
            place_scr[24 * la : 24 * la + 24, 128 * pair : 128 * pair + 128] = jnp.where(
                left, first, second
            )
    high, low = split(place_scr[...])
    spread = spread_ref[...]
    high, low = split(dot(high, spread, NN) + dot(low, spread, NN))
    stack = stack_ref[...]
    out_ref[...] = dot(stack, high, NN) + dot(stack, low, NN)


def call(kernel, outs, spaces, scratch, name):
    smem = pl.BlockSpec(memory_space=pltpu.SMEM)
    vmem = pl.BlockSpec(memory_space=pltpu.VMEM)
    shapes = [pltpu.VMEM(shape, F32) for shape in outs]
    if name == "assemble":
        shapes = [jax.ShapeDtypeStruct(outs[0], F32)]
    run = pl.pallas_call(
        kernel,
        out_shape=shapes if len(shapes) > 1 else shapes[0],
        in_specs=[smem if space == "s" else vmem for space in spaces],
        out_specs=[vmem] * len(shapes) if len(shapes) > 1 else vmem,
        scratch_shapes=[pltpu.VMEM(shape, F32) for shape in scratch],
        name=name,
    )

    def placed(*operands):
        return run(
            *[
                value if space == "s" else pltpu.with_memory_space_constraint(value, pltpu.VMEM)
                for space, value in zip(spaces, operands)
            ]
        )

    return placed


def shifted(value, swap, by_x, by_y):
    pairs = []
    for b in range(2):
        for x in range(16):
            for y in range(16):
                to = 256 * (b ^ swap) + 16 * ((x + by_x) % 16) + (y + by_y) % 16
                pairs.append((256 * b + 16 * x + y, to))
    return lax.ppermute(value, ("body", "gx", "gy"), pairs)


def across_tiles(rows):
    buffer = rows.reshape(256, 3, 1, 128).transpose(0, 2, 1, 3).reshape(256, 1, 384)
    buffer = lax.all_to_all(buffer, ("gx", "gy"), split_axis=0, concat_axis=0, tiled=True)
    return buffer.reshape(256, 1, 3, 128).transpose(0, 2, 1, 3).reshape(768, 128)


def local(surface_disp, proj_coords, pair_slave, pair_owner, send_list):
    to_points, to_nodes, spread, stack = tables()
    side = lax.axis_index("body")
    body = side.astype(jnp.int32).reshape(1)
    sign = (2.0 * side.astype(F32) - 1.0).reshape(1)
    surface = surface_disp.reshape(147, 1, 512)
    coords = proj_coords.reshape(2, 36, 2, 128).transpose(1, 2, 0, 3).reshape(144, 128)
    owner = pair_owner.reshape(1, 256)
    outgoing = call(
        gather_kernel, [(768, 128)], "svv", [(256, 512), (2, 512, 128)], "gather"
    )(body, send_list, surface)
    arrived = across_tiles(outgoing)
    packed = call(slave_kernel, [(208, 256)], "vvvvv", [(192, 512)], "slave")(
        surface, pair_slave, coords, owner, to_points
    )
    packed = shifted(packed, 1, 0, 0)
    columns = call(column_kernel, [(512, 128)], "svvvv", [(512, 128)], "columns")(
        body,
        send_list,
        shifted(send_list, 0, 1, 0),
        shifted(send_list, 0, 0, 1),
        shifted(send_list, 0, 1, 1),
    )
    packed, columns = lax.optimization_barrier((packed, columns))
    returning, traction = call(
        pair_kernel,
        [(768, 128), (120, 256)],
        "svv",
        [(192, 256), (2, 7, 40, 256), (256, 256)],
        "pairs",
    )(sign, arrived, packed)
    returned = across_tiles(returning)
    own, rim_x, rim_y, rim_xy = call(
        slave_force_kernel,
        [(168, 512), (168, 128), (24, 512), (24, 128)],
        "vvv",
        [],
        "slave_force",
    )(traction, packed, to_nodes)
    nodal = call(assemble_kernel, [(144, 384)], "v" * 8, [(216, 512)], "assemble")(
        returned,
        columns,
        shifted(own, 1, 0, 0),
        shifted(rim_x, 1, 1, 0),
        shifted(rim_y, 1, 0, 1),
        shifted(rim_xy, 1, 1, 1),
        spread,
        stack,
    )
    return nodal.reshape(1, 3, 48, 384)


def solution(mesh):
    return jax.shard_map(
        local,
        mesh=mesh,
        in_specs=(
            P("body", None, None, ("gx", "gy")),
            P("body", None, None, ("gx", "gy")),
            P("body", ("gx", "gy")),
            P("body", ("gx", "gy"), None),
            P(None, ("gx", "gy"), None),
        ),
        out_specs=P("body", None, "gx", "gy"),
        check_vma=False,
    )
```

```python
import jax
import jax.numpy as jnp
import numpy as np
from jax import lax
from jax.experimental import pallas as pl
from jax.experimental.pallas import tpu as pltpu
from jax.sharding import PartitionSpec as P

SX = 8
SY = 64
TILES = 256
KAPPA = 2.0
SHEAR = 1.0
LOBATTO_POINTS = (
    -1.0,
    -0.830223896278567,
    -0.4688487934707142,
    0.0,
    0.4688487934707142,
    0.830223896278567,
    1.0,
)
GAUSS_POINTS = (
    -0.932469514203152,
    -0.6612093864662645,
    -0.2386191860831969,
    0.2386191860831969,
    0.6612093864662645,
    0.932469514203152,
)
GAUSS_WEIGHTS = (
    0.1713244923791704,
    0.3607615730481386,
    0.467913934572691,
    0.467913934572691,
    0.3607615730481386,
    0.1713244923791704,
)
F32 = jnp.float32
BF16 = jnp.bfloat16
HIGHEST = lax.Precision.HIGHEST
NN = (((1,), (0,)), ((), ()))
NT = (((1,), (1,)), ((), ()))


def lagrange_scales():
    scales = []
    for k in range(7):
        product = 1.0
        for m in range(7):
            if m != k:
                product /= LOBATTO_POINTS[k] - LOBATTO_POINTS[m]
        scales.append(product)
    return scales


def tables():
    points = np.array(LOBATTO_POINTS)
    gauss = np.array(GAUSS_POINTS)
    single = np.ones((6, 7))
    for k in range(7):
        for m in range(7):
            if m != k:
                single[:, k] *= (gauss - points[m]) / (points[k] - points[m])
    basis = np.einsum("ak,bm->abkm", single, single).reshape(36, 49)
    to_points = np.zeros((120, 192), np.float32)
    to_nodes = np.zeros((192, 120), np.float32)
    for c in range(3):
        to_points[40 * c : 40 * c + 36, 49 * c : 49 * c + 49] = basis
    for row in range(192):
        c, k, m = node_of_row(row)
        to_nodes[row, 40 * c : 40 * c + 36] = basis[:, 7 * k + m]
    spread = np.zeros((512, 384), np.float32)
    for g in range(8):
        for lc in range(64):
            y = 6 * lc + g if g < 7 else (0 if lc == 63 else -1)
            if 0 <= y < 384:
                spread[64 * g + lc, y] = 1.0
    stack = np.zeros((144, 216), np.float32)
    for la in range(9):
        for j in range(24):
            if la < 8 and j < 21:
                c, x = j // 7, 6 * la + j % 7
            elif la == 8 and j >= 21:
                c, x = j - 21, 0
            else:
                continue
            if x < 48:
                stack[48 * c + x, 24 * la + j] = 1.0
    return (
        jnp.asarray(to_points),
        jnp.asarray(to_nodes),
        jnp.asarray(spread, BF16),
        jnp.asarray(stack, BF16),
    )


def node_of_row(row):
    g, j = divmod(row, 24)
    m = min(g, 6)
    if j < 21:
        return j // 7, j % 7, m
    return j - 21, 6, m


def rows_of_node(c, k, m):
    rows = [24 * m + 7 * c + k]
    if k == 6:
        rows.append(24 * m + 21 + c)
    if m == 6:
        rows.append(168 + 7 * c + k)
    if k == 6 and m == 6:
        rows.append(189 + c)
    return rows


def split(value):
    high = value.astype(BF16)
    return high, (value - high.astype(F32)).astype(BF16)


def dot(a, b, dims):
    return lax.dot_general(a, b, dims, preferred_element_type=F32)


def onehot(condition):
    return jnp.where(condition, 1.0, 0.0).astype(BF16)


def iota(shape, dim):
    return lax.broadcasted_iota(jnp.int32, shape, dim)


def third(i):
    return pl.ds(i, 256, stride=3)


def load_surface(surf_ref, scratch):
    flat_ref = surf_ref.reshape(588, 128)
    scratch[144:, :] = jnp.zeros((scratch.shape[0] - 144, 512), F32)
    for j in range(4):
        scratch[0:147, 128 * j : 128 * j + 128] = flat_ref[pl.ds(j, 147, stride=4), :]


def gather_kernel(body_ref, list_ref, surf_ref, out_ref, surf_scr, rows_scr):
    mine = jnp.where(body_ref[0] == 0, list_ref[0], list_ref[1])
    column = jnp.transpose(jnp.broadcast_to(mine.astype(F32), (8, 512)))[:, 0:1]
    pick = onehot(column.astype(jnp.int32) == iota((512, 512), 1))
    load_surface(surf_ref, surf_scr)
    high, low = split(surf_scr[...])
    rows = dot(pick, high, NT) + dot(pick, low, NT)
    rows_scr[0] = rows[:, :128]
    rows_scr[1] = rows[:, 128:]
    left = iota((256, 128), 1) < 64
    out_ref[third(0), :] = rows_scr[0, pl.ds(0, 256, stride=2), :]
    out_ref[third(1), :] = rows_scr[0, pl.ds(1, 256, stride=2), :]
    out_ref[third(2), :] = jnp.where(
        left,
        rows_scr[1, pl.ds(0, 256, stride=2), :],
        pltpu.roll(rows_scr[1, pl.ds(1, 256, stride=2), :], 64, 1),
    )


def slave_kernel(surf_ref, slave_ref, coord_ref, owner_ref, table_ref, out_ref, surf_scr):
    load_surface(surf_ref, surf_scr)
    at_points = lax.dot_general(
        table_ref[...], surf_scr[...], NN, precision=HIGHEST, preferred_element_type=F32
    )
    pick = onehot(iota((512, 256), 0) == slave_ref[...])
    high, low = split(at_points)
    out_ref[0:120, :] = dot(high, pick, NN) + dot(low, pick, NN)
    out_ref[120:200, :] = jnp.zeros((80, 256), F32)
    for e in range(2):
        for j in range(2):
            out_ref[120 + 40 * e : 156 + 40 * e, 128 * j : 128 * j + 128] = coord_ref[
                pl.ds(2 * j + e, 36, stride=4), :
            ]
    out_ref[200:208, :] = jnp.where(
        iota((8, 256), 0) == 0, owner_ref[...], slave_ref[...]
    ).astype(F32)


def unpack(buffer_ref):
    turned = [jnp.transpose(buffer_ref[third(i), :]) for i in range(3)]
    return (
        jnp.concatenate([turned[0], turned[2][:64]], axis=0),
        jnp.concatenate([turned[1], turned[2][64:]], axis=0),
    )


def prepare_kernel(pack_ref, basis_ref, pick_ref):
    owner = pack_ref[200:201, :].astype(jnp.int32)
    named = owner == iota((256, 256), 0)
    pick = onehot(named)
    earlier = onehot(iota((256, 256), 0) < iota((256, 256), 1))
    before = dot(pick, earlier, NN)
    pick_ref[0] = onehot(named & (before < 0.5))
    pick_ref[1] = onehot(named & (before > 0.5))
    scales = lagrange_scales()
    for e in range(2):
        coord = pack_ref[120 + 40 * e : 160 + 40 * e, :]
        parts = [coord - point for point in LOBATTO_POINTS]
        prefix = [None, parts[0]]
        for i in range(1, 6):
            prefix.append(prefix[-1] * parts[i])
        suffix = [None] * 7
        suffix[5] = parts[6]
        for i in range(4, -1, -1):
            suffix[i] = suffix[i + 1] * parts[i + 1]
        for k in range(7):
            if k == 0:
                value = suffix[0]
            elif k == 6:
                value = prefix[6]
            else:
                value = prefix[k] * suffix[k]
            basis_ref[e, k] = value * scales[k]


def pair_kernel(
    sign_ref,
    buffer_ref,
    pack_ref,
    basis_scr,
    pick_ref,
    out_ref,
    traction_ref,
    master_scr,
    force_scr,
):
    sign = sign_ref[0]
    picks = [pick_ref[0], pick_ref[1]]
    master = jnp.zeros((192, 256), F32)
    for half, chosen in zip(unpack(buffer_ref), picks):
        high, low = split(half)
        master = master + dot(high, chosen, NN) + dot(low, chosen, NN)
    master_scr[...] = master
    point = iota((8, 128), 0)
    for t in range(5):
        q = point + 8 * t
        a = jnp.zeros((8, 128), jnp.int32)
        for i in range(1, 6):
            a = a + jnp.where(q >= 6 * i, 1, 0)
        b = q - 6 * a
        weight = jnp.ones((8, 128), F32)
        for index in (a, b):
            near = jnp.where(index > 2, 5 - index, index)
            weight = weight * jnp.where(
                near == 0,
                GAUSS_WEIGHTS[0],
                jnp.where(near == 1, GAUSS_WEIGHTS[1], GAUSS_WEIGHTS[2]),
            )
        weight = jnp.where(q < 36, weight, 0.0)
        rows = slice(8 * t, 8 * t + 8)
        for j in range(2):
            lanes = slice(128 * j, 128 * j + 128)
            first = [basis_scr[0, k, rows, lanes] for k in range(7)]
            second = [basis_scr[1, k, rows, lanes] for k in range(7)]
            for c in range(3):
                total = None
                for k in range(7):
                    inner = None
                    for m in range(7):
                        i = 49 * c + 7 * k + m
                        term = second[m] * master_scr[i : i + 1, lanes]
                        inner = term if inner is None else inner + term
                    inner = first[k] * inner
                    total = inner if total is None else total + inner
                offset = total - pack_ref[40 * c + 8 * t : 40 * c + 8 * t + 8, lanes]
                if c < 2:
                    traction = SHEAR * offset
                else:
                    v = -(sign * offset)
                    pressure = jnp.maximum(v, 0.0) + jnp.log1p(jnp.exp(-jnp.abs(v)))
                    traction = -sign * (KAPPA * pressure)
                traction_ref[40 * c + 8 * t : 40 * c + 8 * t + 8, lanes] = weight * traction
    force_scr[192:256, :] = jnp.zeros((64, 256), F32)
    for j in range(2):
        lanes = slice(128 * j, 128 * j + 128)
        for k in range(7):
            first = basis_scr[0, k, :, lanes]
            weighted = [-first * traction_ref[40 * c : 40 * c + 40, lanes] for c in range(3)]
            for m in range(7):
                second = basis_scr[1, m, :, lanes]
                for c in range(3):
                    row = jnp.sum(weighted[c] * second, axis=0, keepdims=True)
                    for at in rows_of_node(c, k, m):
                        force_scr[at : at + 1, lanes] = row
    high, low = split(force_scr[...])
    to_owner = [dot(chosen, high, NT) + dot(chosen, low, NT) for chosen in picks]
    lane = iota((256, 128), 1)
    row = iota((256, 128), 0)
    wrap = (row & 15) == 0

    def shift_x(value):
        return jnp.concatenate([value[240:], value[:240]], axis=0)

    def shift_y(value):
        return jnp.where(wrap, pltpu.roll(value, 241, 0), pltpu.roll(value, 1, 0))

    rim = jnp.zeros((256, 128), jnp.bool_)
    for g in range(6):
        rim = rim | ((lane >= 24 * g + 21) & (lane < 24 * g + 24))
    tails = []
    for r in range(2):
        head = to_owner[r][:, :128]
        out_ref[third(r), :] = jnp.where(rim, shift_x(head), head)
        tail = to_owner[r][:, 128:]
        tail = jnp.where(lane >= 40, shift_y(tail), tail)
        edge = ((lane >= 13) & (lane < 16)) | ((lane >= 37) & (lane < 40)) | (lane >= 61)
        tails.append(jnp.where(edge, shift_x(tail), tail))
    out_ref[third(2), :] = jnp.where(lane < 64, tails[0], pltpu.roll(tails[1], 64, 1))


def slave_force_kernel(traction_ref, pack_ref, table_ref, own_ref, x_ref, y_ref, xy_ref):
    force = lax.dot_general(
        table_ref[...], traction_ref[...], NN, precision=HIGHEST, preferred_element_type=F32
    )
    pick = onehot(iota((512, 256), 0) == pack_ref[201:202, :].astype(jnp.int32))
    high, low = split(force)
    element = dot(high, pick, NT) + dot(low, pick, NT)
    own_ref[...] = element[:168]
    x_ref[...] = element[:168, 384:]
    y_ref[...] = element[168:]
    xy_ref[...] = element[168:, 384:]


def column_kernel(
    body_ref, list_ref, list_x_ref, list_y_ref, list_xy_ref, out_ref, column_scr
):
    on_first = body_ref[0] == 0
    sub = iota((8, 512), 0)
    lists = jnp.zeros((8, 512), jnp.int32)
    for i, ref in enumerate((list_ref, list_x_ref, list_y_ref, list_xy_ref)):
        lists = jnp.where(sub == i, jnp.where(on_first, ref[0], ref[1]), lists)
    column_scr[:, 0:8] = jnp.transpose(lists.astype(F32))
    for r in range(2):
        out_ref[256 * r : 256 * r + 256, :] = column_scr[pl.ds(r, 256, stride=2), :]


def assemble_kernel(
    buffer_ref,
    column_ref,
    own_ref,
    x_ref,
    y_ref,
    xy_ref,
    spread_ref,
    stack_ref,
    out_ref,
    place_scr,
):
    columns = column_ref[:, 0:8].astype(jnp.int32)
    near = iota((512, 512), 1)
    far = iota((512, 128), 1)
    far = jnp.where(far < 64, far + 448, -1)
    halves = unpack(buffer_ref)
    element = []
    for i, rows in ((0, slice(0, 168)), (2, slice(168, 192))):
        data = jnp.concatenate([half[rows] for half in halves], axis=1)
        high, low = split(data)
        inside = onehot(columns[:, i : i + 1] == near)
        outside = onehot(columns[:, i + 1 : i + 2] == far)
        element.append(
            (
                dot(high, inside, NN) + dot(low, inside, NN),
                dot(high, outside, NN) + dot(low, outside, NN),
            )
        )
    inside = jnp.concatenate([element[0][0] + own_ref[...], element[1][0] + y_ref[...]], axis=0)
    outside = jnp.concatenate(
        [
            element[0][1] + pltpu.roll(x_ref[...], 64, 1),
            element[1][1] + pltpu.roll(xy_ref[...], 64, 1),
        ],
        axis=0,
    )
    left = iota((24, 128), 1) < 64
    for la in range(9):
        if la == 8:
            block = outside
        else:
            block = inside[:, 128 * (la // 2) : 128 * (la // 2) + 128]
        for pair in range(4):
            first = block[48 * pair : 48 * pair + 24]
            second = block[48 * pair + 24 : 48 * pair + 48]
            if la % 2 == 0:
                second = pltpu.roll(second, 64, 1)
            else:
                first = pltpu.roll(first, 64, 1)
            place_scr[24 * la : 24 * la + 24, 128 * pair : 128 * pair + 128] = jnp.where(
                left, first, second
            )
    high, low = split(place_scr[...])
    spread = spread_ref[...]
    high, low = split(dot(high, spread, NN) + dot(low, spread, NN))
    stack = stack_ref[...]
    out_ref[...] = dot(stack, high, NN) + dot(stack, low, NN)


def call(kernel, outs, spaces, scratch, name, types=None):
    smem = pl.BlockSpec(memory_space=pltpu.SMEM)
    vmem = pl.BlockSpec(memory_space=pltpu.VMEM)
    shapes = [pltpu.VMEM(shape, dtype) for shape, dtype in zip(outs, types or [F32] * len(outs))]
    if name == "assemble":
        shapes = [jax.ShapeDtypeStruct(outs[0], F32)]
    run = pl.pallas_call(
        kernel,
        out_shape=shapes if len(shapes) > 1 else shapes[0],
        in_specs=[smem if space == "s" else vmem for space in spaces],
        out_specs=[vmem] * len(shapes) if len(shapes) > 1 else vmem,
        scratch_shapes=[pltpu.VMEM(shape, F32) for shape in scratch],
        name=name,
    )

    def placed(*operands):
        return run(
            *[
                value if space == "s" or name == "gather" else pltpu.with_memory_space_constraint(value, pltpu.VMEM)
                for space, value in zip(spaces, operands)
            ]
        )

    return placed


def shifted(value, swap, by_x, by_y):
    pairs = []
    for b in range(2):
        for x in range(16):
            for y in range(16):
                to = 256 * (b ^ swap) + 16 * ((x + by_x) % 16) + (y + by_y) % 16
                pairs.append((256 * b + 16 * x + y, to))
    return lax.ppermute(value, ("body", "gx", "gy"), pairs)


def across_tiles(rows):
    buffer = rows.reshape(256, 3, 1, 128).transpose(0, 2, 1, 3).reshape(256, 1, 384)
    buffer = lax.all_to_all(buffer, ("gx", "gy"), split_axis=0, concat_axis=0, tiled=True)
    return buffer.reshape(256, 1, 3, 128).transpose(0, 2, 1, 3).reshape(768, 128)


def local(surface_disp, proj_coords, pair_slave, pair_owner, send_list):
    to_points, to_nodes, spread, stack = tables()
    side = lax.axis_index("body")
    body = side.astype(jnp.int32).reshape(1)
    sign = (2.0 * side.astype(F32) - 1.0).reshape(1)
    surface = surface_disp.reshape(147, 1, 512)
    coords = proj_coords.reshape(2, 36, 2, 128).transpose(1, 2, 0, 3).reshape(144, 128)
    owner = pair_owner.reshape(1, 256)
    outgoing = call(
        gather_kernel, [(768, 128)], "svv", [(256, 512), (2, 512, 128)], "gather"
    )(body, send_list, surface)
    arrived = across_tiles(outgoing)
    packed = call(slave_kernel, [(208, 256)], "vvvvv", [(192, 512)], "slave")(
        surface, pair_slave, coords, owner, to_points
    )
    packed = shifted(packed, 1, 0, 0)
    columns = call(column_kernel, [(512, 128)], "svvvv", [(512, 128)], "columns")(
        body,
        send_list,
        shifted(send_list, 0, 1, 0),
        shifted(send_list, 0, 0, 1),
        shifted(send_list, 0, 1, 1),
    )
    basis, picks = call(
        prepare_kernel,
        [(2, 7, 40, 256), (2, 256, 256)],
        "v",
        [],
        "prepare",
        [F32, BF16],
    )(packed)
    basis, columns = lax.optimization_barrier((basis, columns))
    returning, traction = call(
        pair_kernel,
        [(768, 128), (120, 256)],
        "svvvv",
        [(192, 256), (256, 256)],
        "pairs",
    )(sign, arrived, packed, basis, picks)
    returned = across_tiles(returning)
    own, rim_x, rim_y, rim_xy = call(
        slave_force_kernel,
        [(168, 512), (168, 128), (24, 512), (24, 128)],
        "vvv",
        [],
        "slave_force",
    )(traction, packed, to_nodes)
    nodal = call(assemble_kernel, [(144, 384)], "v" * 8, [(216, 512)], "assemble")(
        returned,
        columns,
        shifted(own, 1, 0, 0),
        shifted(rim_x, 1, 1, 0),
        shifted(rim_y, 1, 0, 1),
        shifted(rim_xy, 1, 1, 1),
        spread,
        stack,
    )
    return nodal.reshape(1, 3, 48, 384)


def solution(mesh):
    return jax.shard_map(
        local,
        mesh=mesh,
        in_specs=(
            P("body", None, None, ("gx", "gy")),
            P("body", None, None, ("gx", "gy")),
            P("body", ("gx", "gy")),
            P("body", ("gx", "gy"), None),
            P(None, ("gx", "gy"), None),
        ),
        out_specs=P("body", None, "gx", "gy"),
        check_vma=False,
    )
```

```python
import jax
import jax.numpy as jnp
import numpy as np
from jax import lax
from jax.experimental import pallas as pl
from jax.experimental.pallas import tpu as pltpu
from jax.sharding import PartitionSpec as P

SX = 8
SY = 64
TILES = 256
KAPPA = 2.0
SHEAR = 1.0
LOBATTO_POINTS = (
    -1.0,
    -0.830223896278567,
    -0.4688487934707142,
    0.0,
    0.4688487934707142,
    0.830223896278567,
    1.0,
)
GAUSS_POINTS = (
    -0.932469514203152,
    -0.6612093864662645,
    -0.2386191860831969,
    0.2386191860831969,
    0.6612093864662645,
    0.932469514203152,
)
GAUSS_WEIGHTS = (
    0.1713244923791704,
    0.3607615730481386,
    0.467913934572691,
    0.467913934572691,
    0.3607615730481386,
    0.1713244923791704,
)
F32 = jnp.float32
BF16 = jnp.bfloat16
HIGHEST = lax.Precision.HIGHEST
NN = (((1,), (0,)), ((), ()))
NT = (((1,), (1,)), ((), ()))


def lagrange_scales():
    scales = []
    for k in range(7):
        product = 1.0
        for m in range(7):
            if m != k:
                product /= LOBATTO_POINTS[k] - LOBATTO_POINTS[m]
        scales.append(product)
    return scales


def tables():
    points = np.array(LOBATTO_POINTS)
    gauss = np.array(GAUSS_POINTS)
    single = np.ones((6, 7))
    for k in range(7):
        for m in range(7):
            if m != k:
                single[:, k] *= (gauss - points[m]) / (points[k] - points[m])
    basis = np.einsum("ak,bm->abkm", single, single).reshape(36, 49)
    to_points = np.zeros((120, 192), np.float32)
    to_nodes = np.zeros((192, 120), np.float32)
    for c in range(3):
        to_points[40 * c : 40 * c + 36, 49 * c : 49 * c + 49] = basis
    for row in range(192):
        c, k, m = node_of_row(row)
        to_nodes[row, 40 * c : 40 * c + 36] = basis[:, 7 * k + m]
    spread = np.zeros((512, 384), np.float32)
    for g in range(8):
        for lc in range(64):
            y = 6 * lc + g if g < 7 else (0 if lc == 63 else -1)
            if 0 <= y < 384:
                spread[64 * g + lc, y] = 1.0
    stack = np.zeros((144, 216), np.float32)
    for la in range(9):
        for j in range(24):
            if la < 8 and j < 21:
                c, x = j // 7, 6 * la + j % 7
            elif la == 8 and j >= 21:
                c, x = j - 21, 0
            else:
                continue
            if x < 48:
                stack[48 * c + x, 24 * la + j] = 1.0
    return (
        jnp.asarray(to_points),
        jnp.asarray(to_nodes),
        jnp.asarray(spread, BF16),
        jnp.asarray(stack, BF16),
    )


def node_of_row(row):
    g, j = divmod(row, 24)
    m = min(g, 6)
    if j < 21:
        return j // 7, j % 7, m
    return j - 21, 6, m


def rows_of_node(c, k, m):
    rows = [24 * m + 7 * c + k]
    if k == 6:
        rows.append(24 * m + 21 + c)
    if m == 6:
        rows.append(168 + 7 * c + k)
    if k == 6 and m == 6:
        rows.append(189 + c)
    return rows


def split(value):
    high = value.astype(BF16)
    return high, (value - high.astype(F32)).astype(BF16)


def dot(a, b, dims):
    return lax.dot_general(a, b, dims, preferred_element_type=F32)


def onehot(condition):
    return jnp.where(condition, 1.0, 0.0).astype(BF16)


def iota(shape, dim):
    return lax.broadcasted_iota(jnp.int32, shape, dim)


def third(i):
    return pl.ds(i, 256, stride=3)


def load_surface(surf_ref, scratch):
    flat_ref = surf_ref.reshape(588, 128)
    scratch[144:, :] = jnp.zeros((scratch.shape[0] - 144, 512), F32)
    for j in range(4):
        scratch[0:147, 128 * j : 128 * j + 128] = flat_ref[pl.ds(j, 147, stride=4), :]


def gather_kernel(body_ref, list_ref, surf_ref, out_ref, surf_scr, rows_scr):
    mine = jnp.where(body_ref[0] == 0, list_ref[0], list_ref[1])
    column = jnp.transpose(jnp.broadcast_to(mine.astype(F32), (8, 512)))[:, 0:1]
    pick = onehot(column.astype(jnp.int32) == iota((512, 512), 1))
    load_surface(surf_ref, surf_scr)
    high, low = split(surf_scr[...])
    rows = dot(pick, high, NT) + dot(pick, low, NT)
    rows_scr[0] = rows[:, :128]
    rows_scr[1] = rows[:, 128:]
    left = iota((256, 128), 1) < 64
    out_ref[third(0), :] = rows_scr[0, pl.ds(0, 256, stride=2), :]
    out_ref[third(1), :] = rows_scr[0, pl.ds(1, 256, stride=2), :]
    out_ref[third(2), :] = jnp.where(
        left,
        rows_scr[1, pl.ds(0, 256, stride=2), :],
        pltpu.roll(rows_scr[1, pl.ds(1, 256, stride=2), :], 64, 1),
    )


def slave_kernel(surf_ref, slave_ref, coord_ref, owner_ref, table_ref, out_ref, surf_scr):
    load_surface(surf_ref, surf_scr)
    at_points = lax.dot_general(
        table_ref[...], surf_scr[...], NN, precision=HIGHEST, preferred_element_type=F32
    )
    pick = onehot(iota((512, 256), 0) == slave_ref[...])
    high, low = split(at_points)
    out_ref[0:120, :] = dot(high, pick, NN) + dot(low, pick, NN)
    out_ref[120:200, :] = jnp.zeros((80, 256), F32)
    for e in range(2):
        for j in range(2):
            out_ref[120 + 40 * e : 156 + 40 * e, 128 * j : 128 * j + 128] = coord_ref[
                pl.ds(2 * j + e, 36, stride=4), :
            ]
    out_ref[200:208, :] = jnp.where(
        iota((8, 256), 0) == 0, owner_ref[...], slave_ref[...]
    ).astype(F32)


def unpack(buffer_ref):
    turned = [jnp.transpose(buffer_ref[third(i), :]) for i in range(3)]
    return (
        jnp.concatenate([turned[0], turned[2][:64]], axis=0),
        jnp.concatenate([turned[1], turned[2][64:]], axis=0),
    )


def prepare_kernel(pack_ref, basis_ref, pick_ref):
    owner = pack_ref[200:201, :].astype(jnp.int32)
    named = owner == iota((256, 256), 0)
    pick = onehot(named)
    earlier = onehot(iota((256, 256), 0) < iota((256, 256), 1))
    before = dot(pick, earlier, NN)
    pick_ref[0] = onehot(named & (before < 0.5))
    pick_ref[1] = onehot(named & (before > 0.5))
    scales = lagrange_scales()
    for e in range(2):
        coord = pack_ref[120 + 40 * e : 160 + 40 * e, :]
        parts = [coord - point for point in LOBATTO_POINTS]
        prefix = [None, parts[0]]
        for i in range(1, 6):
            prefix.append(prefix[-1] * parts[i])
        suffix = [None] * 7
        suffix[5] = parts[6]
        for i in range(4, -1, -1):
            suffix[i] = suffix[i + 1] * parts[i + 1]
        for k in range(7):
            if k == 0:
                value = suffix[0]
            elif k == 6:
                value = prefix[6]
            else:
                value = prefix[k] * suffix[k]
            basis_ref[e, k] = value * scales[k]


def pair_kernel(
    sign_ref,
    buffer_ref,
    pack_ref,
    basis_scr,
    pick_ref,
    out_ref,
    traction_ref,
    master_scr,
    force_scr,
):
    sign = sign_ref[0]
    picks = [pick_ref[0], pick_ref[1]]
    master = jnp.zeros((192, 256), F32)
    for half, chosen in zip(unpack(buffer_ref), picks):
        high, low = split(half)
        master = master + dot(high, chosen, NN) + dot(low, chosen, NN)
    master_scr[...] = master
    point = iota((8, 128), 0)
    for t in range(5):
        q = point + 8 * t
        a = jnp.zeros((8, 128), jnp.int32)
        for i in range(1, 6):
            a = a + jnp.where(q >= 6 * i, 1, 0)
        b = q - 6 * a
        weight = jnp.ones((8, 128), F32)
        for index in (a, b):
            near = jnp.where(index > 2, 5 - index, index)
            weight = weight * jnp.where(
                near == 0,
                GAUSS_WEIGHTS[0],
                jnp.where(near == 1, GAUSS_WEIGHTS[1], GAUSS_WEIGHTS[2]),
            )
        weight = jnp.where(q < 36, weight, 0.0)
        rows = slice(8 * t, 8 * t + 8)
        for j in range(2):
            lanes = slice(128 * j, 128 * j + 128)
            first = [basis_scr[0, k, rows, lanes] for k in range(7)]
            second = [basis_scr[1, k, rows, lanes] for k in range(7)]
            for c in range(3):
                total = None
                for k in range(7):
                    inner = None
                    for m in range(7):
                        i = 49 * c + 7 * k + m
                        term = second[m] * master_scr[i : i + 1, lanes]
                        inner = term if inner is None else inner + term
                    inner = first[k] * inner
                    total = inner if total is None else total + inner
                offset = total - pack_ref[40 * c + 8 * t : 40 * c + 8 * t + 8, lanes]
                if c < 2:
                    traction = SHEAR * offset
                else:
                    v = -(sign * offset)
                    pressure = jnp.maximum(v, 0.0) + jnp.log1p(jnp.exp(-jnp.abs(v)))
                    traction = -sign * (KAPPA * pressure)
                traction_ref[40 * c + 8 * t : 40 * c + 8 * t + 8, lanes] = weight * traction
    force_scr[192:256, :] = jnp.zeros((64, 256), F32)
    for j in range(2):
        lanes = slice(128 * j, 128 * j + 128)
        for k in range(7):
            first = basis_scr[0, k, :, lanes]
            weighted = [-first * traction_ref[40 * c : 40 * c + 40, lanes] for c in range(3)]
            for m in range(7):
                second = basis_scr[1, m, :, lanes]
                for c in range(3):
                    row = jnp.sum(weighted[c] * second, axis=0, keepdims=True)
                    for at in rows_of_node(c, k, m):
                        force_scr[at : at + 1, lanes] = row
    high, low = split(force_scr[...])
    to_owner = [dot(chosen, high, NT) + dot(chosen, low, NT) for chosen in picks]
    lane = iota((256, 128), 1)
    row = iota((256, 128), 0)
    wrap = (row & 15) == 0

    def shift_x(value):
        return jnp.concatenate([value[240:], value[:240]], axis=0)

    def shift_y(value):
        return jnp.where(wrap, pltpu.roll(value, 241, 0), pltpu.roll(value, 1, 0))

    rim = jnp.zeros((256, 128), jnp.bool_)
    for g in range(6):
        rim = rim | ((lane >= 24 * g + 21) & (lane < 24 * g + 24))
    tails = []
    for r in range(2):
        head = to_owner[r][:, :128]
        out_ref[third(r), :] = jnp.where(rim, shift_x(head), head)
        tail = to_owner[r][:, 128:]
        tail = jnp.where(lane >= 40, shift_y(tail), tail)
        edge = ((lane >= 13) & (lane < 16)) | ((lane >= 37) & (lane < 40)) | (lane >= 61)
        tails.append(jnp.where(edge, shift_x(tail), tail))
    out_ref[third(2), :] = jnp.where(lane < 64, tails[0], pltpu.roll(tails[1], 64, 1))


def slave_force_kernel(
    traction_ref, pack_ref, table_ref, column_ref, own_ref, x_ref, y_ref, xy_ref, hot_ref
):
    columns = column_ref[:, 0:8].astype(jnp.int32)
    near = iota((512, 512), 1)
    far = iota((512, 128), 1)
    far = jnp.where(far < 64, far + 448, -1)
    for i in (0, 2):
        hot_ref[:, 320 * i : 320 * i + 512] = onehot(columns[:, i : i + 1] == near)
        hot_ref[:, 320 * i + 512 : 320 * i + 640] = onehot(columns[:, i + 1 : i + 2] == far)
    force = lax.dot_general(
        table_ref[...], traction_ref[...], NN, precision=HIGHEST, preferred_element_type=F32
    )
    pick = onehot(iota((512, 256), 0) == pack_ref[201:202, :].astype(jnp.int32))
    high, low = split(force)
    element = dot(high, pick, NT) + dot(low, pick, NT)
    own_ref[...] = element[:168]
    x_ref[...] = element[:168, 384:]
    y_ref[...] = element[168:]
    xy_ref[...] = element[168:, 384:]


def column_kernel(
    body_ref, list_ref, list_x_ref, list_y_ref, list_xy_ref, out_ref, column_scr
):
    on_first = body_ref[0] == 0
    sub = iota((8, 512), 0)
    lists = jnp.zeros((8, 512), jnp.int32)
    for i, ref in enumerate((list_ref, list_x_ref, list_y_ref, list_xy_ref)):
        lists = jnp.where(sub == i, jnp.where(on_first, ref[0], ref[1]), lists)
    column_scr[:, 0:8] = jnp.transpose(lists.astype(F32))
    for r in range(2):
        out_ref[256 * r : 256 * r + 256, :] = column_scr[pl.ds(r, 256, stride=2), :]


def assemble_kernel(
    buffer_ref,
    hot_ref,
    own_ref,
    x_ref,
    y_ref,
    xy_ref,
    spread_ref,
    stack_ref,
    out_ref,
    place_scr,
):
    halves = unpack(buffer_ref)
    element = []
    for i, rows in ((0, slice(0, 168)), (2, slice(168, 192))):
        data = jnp.concatenate([half[rows] for half in halves], axis=1)
        high, low = split(data)
        inside = hot_ref[:, 320 * i : 320 * i + 512]
        outside = hot_ref[:, 320 * i + 512 : 320 * i + 640]
        element.append(
            (
                dot(high, inside, NN) + dot(low, inside, NN),
                dot(high, outside, NN) + dot(low, outside, NN),
            )
        )
    inside = jnp.concatenate([element[0][0] + own_ref[...], element[1][0] + y_ref[...]], axis=0)
    outside = jnp.concatenate(
        [
            element[0][1] + pltpu.roll(x_ref[...], 64, 1),
            element[1][1] + pltpu.roll(xy_ref[...], 64, 1),
        ],
        axis=0,
    )
    left = iota((24, 128), 1) < 64
    for la in range(9):
        if la == 8:
            block = outside
        else:
            block = inside[:, 128 * (la // 2) : 128 * (la // 2) + 128]
        for pair in range(4):
            first = block[48 * pair : 48 * pair + 24]
            second = block[48 * pair + 24 : 48 * pair + 48]
            if la % 2 == 0:
                second = pltpu.roll(second, 64, 1)
            else:
                first = pltpu.roll(first, 64, 1)
            place_scr[24 * la : 24 * la + 24, 128 * pair : 128 * pair + 128] = jnp.where(
                left, first, second
            )
    high, low = split(place_scr[...])
    spread = spread_ref[...]
    high, low = split(dot(high, spread, NN) + dot(low, spread, NN))
    stack = stack_ref[...]
    out_ref[...] = dot(stack, high, NN) + dot(stack, low, NN)


def call(kernel, outs, spaces, scratch, name, types=None):
    smem = pl.BlockSpec(memory_space=pltpu.SMEM)
    vmem = pl.BlockSpec(memory_space=pltpu.VMEM)
    shapes = [pltpu.VMEM(shape, dtype) for shape, dtype in zip(outs, types or [F32] * len(outs))]
    if name == "assemble":
        shapes = [jax.ShapeDtypeStruct(outs[0], F32)]
    run = pl.pallas_call(
        kernel,
        out_shape=shapes if len(shapes) > 1 else shapes[0],
        in_specs=[smem if space == "s" else vmem for space in spaces],
        out_specs=[vmem] * len(shapes) if len(shapes) > 1 else vmem,
        scratch_shapes=[pltpu.VMEM(shape, F32) for shape in scratch],
        name=name,
    )

    def placed(*operands):
        return run(
            *[
                value if space == "s" or name == "gather" else pltpu.with_memory_space_constraint(value, pltpu.VMEM)
                for space, value in zip(spaces, operands)
            ]
        )

    return placed


def shifted(value, swap, by_x, by_y):
    pairs = []
    for b in range(2):
        for x in range(16):
            for y in range(16):
                to = 256 * (b ^ swap) + 16 * ((x + by_x) % 16) + (y + by_y) % 16
                pairs.append((256 * b + 16 * x + y, to))
    return lax.ppermute(value, ("body", "gx", "gy"), pairs)


def across_tiles(rows):
    buffer = rows.reshape(256, 3, 1, 128).transpose(0, 2, 1, 3).reshape(256, 1, 384)
    buffer = lax.all_to_all(buffer, ("gx", "gy"), split_axis=0, concat_axis=0, tiled=True)
    return buffer.reshape(256, 1, 3, 128).transpose(0, 2, 1, 3).reshape(768, 128)


def local(surface_disp, proj_coords, pair_slave, pair_owner, send_list):
    to_points, to_nodes, spread, stack = tables()
    side = lax.axis_index("body")
    body = side.astype(jnp.int32).reshape(1)
    sign = (2.0 * side.astype(F32) - 1.0).reshape(1)
    surface = surface_disp.reshape(147, 1, 512)
    coords = proj_coords.reshape(2, 36, 2, 128).transpose(1, 2, 0, 3).reshape(144, 128)
    owner = pair_owner.reshape(1, 256)
    outgoing = call(
        gather_kernel, [(768, 128)], "svv", [(256, 512), (2, 512, 128)], "gather"
    )(body, send_list, surface)
    arrived = across_tiles(outgoing)
    packed = call(slave_kernel, [(208, 256)], "vvvvv", [(192, 512)], "slave")(
        surface, pair_slave, coords, owner, to_points
    )
    packed = shifted(packed, 1, 0, 0)
    columns = call(column_kernel, [(512, 128)], "svvvv", [(512, 128)], "columns")(
        body,
        send_list,
        shifted(send_list, 0, 1, 0),
        shifted(send_list, 0, 0, 1),
        shifted(send_list, 0, 1, 1),
    )
    basis, picks = call(
        prepare_kernel,
        [(2, 7, 40, 256), (2, 256, 256)],
        "v",
        [],
        "prepare",
        [F32, BF16],
    )(packed)
    basis, columns = lax.optimization_barrier((basis, columns))
    returning, traction = call(
        pair_kernel,
        [(768, 128), (120, 256)],
        "svvvv",
        [(192, 256), (256, 256)],
        "pairs",
    )(sign, arrived, packed, basis, picks)
    returned = across_tiles(returning)
    own, rim_x, rim_y, rim_xy, hot = call(
        slave_force_kernel,
        [(168, 512), (168, 128), (24, 512), (24, 128), (512, 1280)],
        "vvvv",
        [],
        "slave_force",
        [F32, F32, F32, F32, BF16],
    )(traction, packed, to_nodes, columns)
    nodal = call(assemble_kernel, [(144, 384)], "v" * 8, [(216, 512)], "assemble")(
        returned,
        hot,
        shifted(own, 1, 0, 0),
        shifted(rim_x, 1, 1, 0),
        shifted(rim_y, 1, 0, 1),
        shifted(rim_xy, 1, 1, 1),
        spread,
        stack,
    )
    return nodal.reshape(1, 3, 48, 384)


def solution(mesh):
    return jax.shard_map(
        local,
        mesh=mesh,
        in_specs=(
            P("body", None, None, ("gx", "gy")),
            P("body", None, None, ("gx", "gy")),
            P("body", ("gx", "gy")),
            P("body", ("gx", "gy"), None),
            P(None, ("gx", "gy"), None),
        ),
        out_specs=P("body", None, "gx", "gy"),
        check_vma=False,
    )
```
